32 devices in a mesh: nodes: 16 (over z, y, x), fsdp: 2 (over core).
Axes of the slice: x: 2, y: 2, z: 4, core: 2. Of those that a mesh axis runs over, the one named last changes fastest.
Arguments:
- features: bfloat16 [49152, 512], P(('nodes', 'fsdp')), may hold values from -6 to 6
- targets: float32 [49152], P(('nodes', 'fsdp')), may hold values from -6 to 6
- node_mask: int32 [49152], P(('nodes', 'fsdp')), may hold values 0 or 1
- block_counts: int32 [32], P(('nodes', 'fsdp')), may hold values from 1 to 12, as said below
- neighbours: int32 [384, 8], P(('nodes', 'fsdp')), may hold values from 0 to 11, as said below
- edge_types: int32 [384, 9], P(('nodes', 'fsdp')), may hold values from 0 to 63
- proj_weights: float32 [5, 512, 512], P(None, ('nodes', 'fsdp'))
- ffn_weights: float32 [2, 512, 2048], P(None, ('nodes', 'fsdp'))
- vector_params: float32 [8, 512], P(None, ('nodes', 'fsdp'))
- proj_mean: float32 [5, 512, 512], P(None, ('nodes', 'fsdp')), may hold values from -0.009765625 to 0.009765625
- ffn_mean: float32 [2, 512, 2048], P(None, ('nodes', 'fsdp')), may hold values from -0.009765625 to 0.009765625
- vector_mean: float32 [8, 512], P(None, ('nodes', 'fsdp')), may hold values from -0.009765625 to 0.009765625
- proj_square: float32 [5, 512, 512], P(None, ('nodes', 'fsdp')), may hold values from 1.0172526e-08 to 1.0172526e-07
- ffn_square: float32 [2, 512, 2048], P(None, ('nodes', 'fsdp')), may hold values from 1.0172526e-08 to 1.0172526e-07
- vector_square: float32 [8, 512], P(None, ('nodes', 'fsdp')), may hold values from 9.765625e-07 to 9.765625e-06
Outputs:
- updated_proj: float32 [5, 512, 512], P(None, ('nodes', 'fsdp'))
- updated_ffn: float32 [2, 512, 2048], P(None, ('nodes', 'fsdp'))
- updated_vector: float32 [8, 512], P(None, ('nodes', 'fsdp'))
- mean_proj: float32 [5, 512, 512], P(None, ('nodes', 'fsdp'))
- mean_ffn: float32 [2, 512, 2048], P(None, ('nodes', 'fsdp'))
- mean_vector: float32 [8, 512], P(None, ('nodes', 'fsdp'))
- square_proj: float32 [5, 512, 512], P(None, ('nodes', 'fsdp'))
- square_ffn: float32 [2, 512, 2048], P(None, ('nodes', 'fsdp'))
- square_vector: float32 [8, 512], P(None, ('nodes', 'fsdp'))
- copy_proj: bfloat16 [5, 512, 512], P(None, ('nodes', 'fsdp'))
- copy_ffn: bfloat16 [2, 512, 2048], P(None, ('nodes', 'fsdp'))
- copy_vector: bfloat16 [8, 512], P(None, ('nodes', 'fsdp'))
- norm_pairs: float32 [15, 2], replicated
- stream_scale: float32 [4], replicated
- train_loss: float32 [], replicated
The draws below stay inside these ranges and needn't reach their ends.
Inputs may be any that keep to these rules, and one draw needn't show every extreme that they name: `block_counts`: live slots of a device come first; one device has 12 live blocks and one has a single live block. `neighbours`: each entry names a live slot of the device it refers to.
All inputs are finite; a program needn't handle non-finite values. No bound on the sum of `node_mask` on one device may be relied on, other than what follows from the above.
Results may differ from the reference program's by a relative error of at most 0.0015.
The reference program's roundings to bfloat16 on the way count: a program that leaves them out, or rounds other values in their place, can miss the bound.
Values may be sent and summed in bfloat16 or wider, within the bound.
No kernel may reach another device: no remote copies, remote signals or barrier semaphores. Data moves between devices by JAX's collectives and lax.ppermute only.
A program may use at most 320 MiB of HBM per device.

```python
import math
import jax
import jax.numpy as jnp
from jax import lax

D = 512
H = 8
HD = 64
FF = 2048
NB = 128
NNB = 8
STEP = 10
BCAP = 12
NTYPES = 64
NRANK = 16
NPAIR = 2
BLOCKS = 384
ROWS = 49152
DEVICES = 32


def count_table(key):
    base_key = jax.random.fold_in(key, 7)
    draw_key, order_key = jax.random.split(base_key)
    drawn = jax.random.randint(draw_key, (DEVICES,), 1, BCAP + 1)
    order = jax.random.permutation(order_key, DEVICES)
    return drawn.at[order[0]].set(BCAP).at[order[1]].set(1).astype(jnp.int32)


def draw_block_counts(key, part):
    return count_table(key)


def draw_neighbours(key, part):
    counted = count_table(key)
    block_ids = jnp.arange(BLOCKS, dtype=jnp.int32)
    device = block_ids // BCAP
    rank_index = device // NPAIR
    pair_index = device % NPAIR
    shifts = jnp.array([1, -1, NRANK // 4, NRANK // 2], dtype=jnp.int32)[jnp.arange(NNB, dtype=jnp.int32) // 2]
    source = (rank_index[:, None] - shifts[None, :]) % NRANK * NPAIR + pair_index[:, None]
    picks = jax.random.randint(jax.random.fold_in(key, 13), (BLOCKS, NNB), 0, 1 << 20)
    return (picks % counted[source]).astype(jnp.int32)


def draw_proj_weights(key, part):
    factors = jnp.array([1.0, 1.0, 1.0, 1.0, 8.0], jnp.float32) * D ** (-0.5)
    return jax.random.normal(key, (5, D, D), jnp.float32) * factors[:, None, None]


def draw_ffn_weights(key, part):
    factors = jnp.array([D ** (-0.5), 1.5 * FF ** (-0.5)], jnp.float32)
    return jax.random.normal(key, (2, D, FF), jnp.float32) * factors[:, None, None]


def draw_vector_params(key, part):
    subkeys = jax.random.split(key, 4)
    gain_rows = jax.random.uniform(subkeys[0], (3, D), jnp.float32, 0.6, 1.4)
    shift_rows = jax.random.uniform(subkeys[1], (3, D), jnp.float32, -0.5, 0.5)
    head_row = jax.random.normal(subkeys[2], (D,), jnp.float32) * D ** (-0.5)
    type_table = jax.random.normal(subkeys[3], (D,), jnp.float32)
    stacked = [gain_rows[0], shift_rows[0], gain_rows[1], shift_rows[1], gain_rows[2], shift_rows[2], head_row, type_table]
    return jnp.stack(stacked)


def place_ends(result, stream_key, smallest, top_value):
    longest = result.shape.index(max(result.shape))
    spots = []
    for shift in (0, 1):
        where = [jax.random.randint(jax.random.fold_in(stream_key, axis), (), 0, length) for axis, length in enumerate(result.shape)]
        where[longest] = (where[longest] + shift) % result.shape[longest]
        spots.append(tuple(where))
    return result.at[spots[0]].set(smallest).at[spots[1]].set(top_value)


def shard_levels(own_key, dims, cuts, least, top_value):
    def one(position, parts):
        steps = jax.random.uniform(jax.random.fold_in(jax.random.fold_in(own_key, 6), position), (parts,), jnp.float32, least / len(cuts), top_value / len(cuts))
        return jnp.repeat(jnp.exp(steps), dims[position] // parts).reshape((-1,) + (1,) * (len(dims) - position - 1))

    factor_of = one(*cuts[0])
    for cut in cuts[1:]:
        factor_of = factor_of * one(*cut)
    return factor_of


def gaussian(own_key, shape, scale, bound, shards=(), held_as=jnp.bfloat16):
    gain = shard_levels(own_key, shape, shards, -0.22, 0.18) if shards else 1.0
    result = jax.random.normal(own_key, shape, jnp.float32) * scale * gain
    return jnp.minimum(jnp.maximum(result, -bound), bound).astype(held_as)


def setup_inputs(seed: int = 0) -> dict:
    key_of = jax.random.split(jax.random.key(seed), 16)
    features = gaussian(key_of[0], (ROWS, D), 1.0, 6.0, ((0, 32),))
    targets = gaussian(key_of[1], (ROWS,), 1.0, 6.0, ((0, 32),), jnp.float32)
    node_mask = place_ends((jax.random.randint(key_of[2], (ROWS,), 0, 8) < 7).astype(jnp.int32), jax.random.fold_in(key_of[2], 1), 0, 1)
    block_counts = draw_block_counts(jax.random.fold_in(key_of[15], 71), 0)
    neighbours = draw_neighbours(jax.random.fold_in(key_of[15], 71), 0)
    edge_types = place_ends(jax.random.randint(key_of[5], (BLOCKS, NNB + 1), 0, NTYPES), jax.random.fold_in(key_of[5], 1), 0, NTYPES - 1).astype(jnp.int32)
    proj_weights = draw_proj_weights(jax.random.fold_in(key_of[15], 71), 0)
    ffn_weights = draw_ffn_weights(jax.random.fold_in(key_of[15], 71), 0)
    vector_params = draw_vector_params(jax.random.fold_in(key_of[15], 71), 0)
    proj_mean = gaussian(key_of[9], (5, D, D), (0.15 * (DEVICES * BCAP * NB) ** -0.5), 0.009765625, ((1, 32),), jnp.float32)
    ffn_mean = gaussian(key_of[10], (2, D, FF), (0.15 * (DEVICES * BCAP * NB) ** -0.5), 0.009765625, ((1, 32),), jnp.float32)
    vector_mean = gaussian(key_of[11], (8, D), (0.15 * (DEVICES * BCAP * NB) ** -0.5), 0.009765625, ((1, 32),), jnp.float32)
    proj_square = jnp.clip(jnp.exp(math.log(1.0172526287988148e-07) - 2.3025851 * jax.random.uniform(key_of[12], (5, D, D), jnp.float32) ** shard_levels(key_of[12], (5, D, D), ((1, 32),), -0.2, 0.2)), 1.017252593271678e-08, 1.0172526287988148e-07)
    ffn_square = jnp.clip(jnp.exp(math.log(1.0172526287988148e-07) - 2.3025851 * jax.random.uniform(key_of[13], (2, D, FF), jnp.float32) ** shard_levels(key_of[13], (2, D, FF), ((1, 32),), -0.2, 0.2)), 1.017252593271678e-08, 1.0172526287988148e-07)
    vector_square = jnp.clip(jnp.exp(math.log(9.765624781721272e-06) - 2.30258502 * jax.random.uniform(key_of[14], (8, D), jnp.float32) ** shard_levels(key_of[14], (8, D), ((1, 32),), -0.2, 0.2)), 9.765625463842298e-07, 9.765624781721272e-06)
    return dict(features=features, targets=targets, node_mask=node_mask, block_counts=block_counts, neighbours=neighbours, edge_types=edge_types, proj_weights=proj_weights, ffn_weights=ffn_weights, vector_params=vector_params, proj_mean=proj_mean, ffn_mean=ffn_mean, vector_mean=vector_mean, proj_square=proj_square, ffn_square=ffn_square, vector_square=vector_square)


@jax.custom_vjp
def low(v):
    return lax.optimization_barrier(v.astype(jnp.bfloat16)).astype(jnp.float32)

@jax.custom_vjp
def low_back(v):
    return v

def low_keep(v):
    return (low(v), None)

def low_pass(kept, grad):
    return (grad,)

def back_keep(v):
    return (v, None)

def back_low(kept, grad):
    return (low(grad),)
low.defvjp(low_keep, low_pass)
low_back.defvjp(back_keep, back_low)
norm_eps = 1e-05
adam_eps = 1e-06
beta_first = 0.9
beta_second = 0.999
decay_rate = 0.01
learn_rate = 0.2
mask_fill = 1000000000.0
precise = lax.Precision.HIGHEST

def layer_norm(values, gain_row, shift_row):
    center = values - lax.optimization_barrier(jnp.mean(values, -1, keepdims=True))
    spread = lax.optimization_barrier(jnp.mean(center * center, -1, keepdims=True))
    return center * lax.rsqrt(spread + norm_eps) * gain_row + shift_row

def attend_group(query, key_part, value_part, key_valid, bias_part, factor):
    raw_scores = low_back(factor * jnp.einsum('bqhd,bjkhd->bhqjk', query, key_part, precision=precise))
    scores = raw_scores + bias_part[:, :, None, :, None] + (key_valid[:, None, None, :, :] - 1.0) * mask_fill
    probs = low(jax.nn.softmax(scores, axis=(3, 4)))
    return jnp.einsum('bhqjk,bjkhd->bqhd', probs, value_part, precision=precise)

def grouped_copies(rows):
    pieces = [rows] + [low_back(rows) for group in range(4)]
    return jnp.concatenate(pieces, 0).reshape(5 * BLOCKS, NB, H, HD)

def forward_pass(proj_w, ffn_w, vector_w, inputs, valid_rows, key_blocks, edge_types, targets, node_total):
    low_proj = low(proj_w)
    low_ffn = low(ffn_w)
    low_vector = low(vector_w)
    base = low_back(jnp.dot(inputs, low_proj[0], precision=precise))
    attn_in = low(layer_norm(base, low_vector[0], low_vector[1]))
    queries = low_back(low(jnp.dot(attn_in, low_proj[1], precision=precise)))
    key_rows = low_back(low(jnp.dot(attn_in, low_proj[2], precision=precise)))
    value_rows = low_back(low(jnp.dot(attn_in, low_proj[3], precision=precise)))
    type_table = low_vector[7].reshape(NTYPES, H)
    factor = HD ** (-0.5)
    query_blocks = queries.reshape(BLOCKS, NB, H, HD)
    key_stack = grouped_copies(key_rows)
    value_stack = grouped_copies(value_rows)
    valid_blocks = valid_rows.reshape(BLOCKS, NB)
    copy_offsets = jnp.concatenate([jnp.zeros((1,), jnp.int32), (1 + jnp.arange(NNB, dtype=jnp.int32) // 2) * BLOCKS])

    def one_group(group_index):
        first_block = group_index * 4
        chosen = lax.dynamic_slice_in_dim(key_blocks, first_block, 4, 0)
        picked = (chosen + copy_offsets[None, :]).astype(jnp.int32)
        query = lax.dynamic_slice_in_dim(query_blocks, first_block, 4, 0)
        kinds = lax.dynamic_slice_in_dim(edge_types, first_block, 4, 0)
        bias_part = jnp.transpose(type_table[kinds], (0, 2, 1))
        return attend_group(query, key_stack[picked], value_stack[picked], valid_blocks[chosen], bias_part, factor)
    attended = lax.map(jax.checkpoint(one_group), jnp.arange(BLOCKS // 4, dtype=jnp.int32))
    attn_rows = low_back(low(attended.reshape(ROWS, D)))
    attn_y = low_back(jnp.dot(attn_rows, low_proj[4], precision=precise))
    middle = base + attn_y
    ffn_in = low(layer_norm(middle, low_vector[2], low_vector[3]))
    hidden_pre = low_back(jnp.dot(ffn_in, low_ffn[0], precision=precise))
    hidden = low(jax.nn.gelu(hidden_pre))
    ffn_y = low_back(jnp.dot(hidden, low_ffn[1].T, precision=precise))
    final = middle + ffn_y
    predict = lax.optimization_barrier(jnp.sum(layer_norm(final, low_vector[4], low_vector[5]) * low_vector[6], -1))
    error = predict - targets
    loss_value = jnp.sum(valid_rows * error * error) / node_total
    squares = jnp.stack([jnp.sum(valid_rows[:, None] * piece * piece) for piece in (middle, attn_y, final, ffn_y)])
    return (loss_value, squares)

def lamb_parts(weight, gradient, moment_one, moment_two, axes_list):
    mean_new = beta_first * moment_one + (1.0 - beta_first) * gradient
    square_new = beta_second * moment_two + (1.0 - beta_second) * gradient * gradient
    corrected = mean_new / (1.0 - beta_first ** STEP) / (jnp.sqrt(square_new / (1.0 - beta_second ** STEP)) + adam_eps)
    direction = corrected + decay_rate * weight
    return (mean_new, square_new, direction, lax.optimization_barrier(jnp.sum(weight * weight, axes_list)), lax.optimization_barrier(jnp.sum(direction * direction, axes_list)))

def reference(features, targets, node_mask, block_counts, neighbours, edge_types, proj_weights, ffn_weights, vector_params, proj_mean, ffn_mean, vector_mean, proj_square, ffn_square, vector_square):
    block_ids = jnp.arange(BLOCKS, dtype=jnp.int32)
    device = block_ids // BCAP
    rank_index = device // NPAIR
    pair_index = device % NPAIR
    shifts = jnp.array([1, -1, NRANK // 4, NRANK // 2], dtype=jnp.int32)[jnp.arange(NNB, dtype=jnp.int32) // 2]
    source = (rank_index[:, None] - shifts[None, :]) % NRANK * NPAIR + pair_index[:, None]
    far_blocks = (source * BCAP + neighbours).astype(jnp.int32)
    key_blocks = jnp.concatenate([block_ids[:, None], far_blocks], 1)
    live_slots = (block_ids % BCAP < block_counts[device]).astype(jnp.float32)
    valid_rows = (node_mask.reshape(BLOCKS, NB).astype(jnp.float32) * live_slots[:, None]).reshape(ROWS)
    node_total = jnp.sum(valid_rows)
    inputs = features.astype(jnp.float32)

    def objective(proj_w, ffn_w, vector_w):
        return forward_pass(proj_w, ffn_w, vector_w, inputs, valid_rows, key_blocks, edge_types, targets, node_total)
    loss_value, pullback, squares = jax.vjp(objective, proj_weights, ffn_weights, vector_params, has_aux=True)
    grad_proj, grad_ffn, grad_vector = pullback(jnp.ones((), jnp.float32))
    proj_parts = lamb_parts(proj_weights, grad_proj, proj_mean, proj_square, (1, 2))
    ffn_parts = lamb_parts(ffn_weights, grad_ffn, ffn_mean, ffn_square, (1, 2))
    vector_parts = lamb_parts(vector_params, grad_vector, vector_mean, vector_square, (1,))
    weight_sq = jnp.concatenate([proj_parts[3], ffn_parts[3], vector_parts[3]])
    direction_sq = jnp.concatenate([proj_parts[4], ffn_parts[4], vector_parts[4]])
    norm_pairs = jnp.sqrt(jnp.stack([weight_sq, direction_sq], 1))
    ratio = norm_pairs[:, 0] / norm_pairs[:, 1]
    updated_proj = proj_weights - learn_rate * ratio[0:5, None, None] * proj_parts[2]
    updated_ffn = ffn_weights - learn_rate * ratio[5:7, None, None] * ffn_parts[2]
    updated_vector = vector_params - learn_rate * ratio[7:15, None] * vector_parts[2]
    stream_scale = jnp.sqrt(squares / (node_total * D))
    return (updated_proj, updated_ffn, updated_vector, proj_parts[0], ffn_parts[0], vector_parts[0], proj_parts[1], ffn_parts[1], vector_parts[1], updated_proj.astype(jnp.bfloat16), updated_ffn.astype(jnp.bfloat16), updated_vector.astype(jnp.bfloat16), norm_pairs, stream_scale, loss_value)
```

```python
import functools
import jax
import jax.numpy as jnp
from jax import lax
from jax.experimental import pallas as pl
from jax.experimental.pallas import tpu as pltpu
from jax.sharding import PartitionSpec as P

H = 8
HD = 64
STEP = 10
NTYPES = 64

norm_eps = 1e-05
adam_eps = 1e-06
beta_first = 0.9
beta_second = 0.999
decay_rate = 0.01
learn_rate = 0.2
mask_fill = 1000000000.0
precise = lax.Precision.HIGHEST
both = ("nodes", "fsdp")
f32 = jnp.float32
bf16 = jnp.bfloat16
scale = HD ** (-0.5)


def passed_along(value, steps):
    count = lax.axis_size("nodes")
    pairs = [(source, (source + steps) % count) for source in range(count)]
    return lax.ppermute(value, "nodes", pairs)


def layer_norm(values, gain_row, shift_row):
    center = values - jnp.mean(values, -1, keepdims=True)
    spread = jnp.mean(center * center, -1, keepdims=True)
    return center * lax.rsqrt(spread + norm_eps) * gain_row + shift_row


def head_out(values, gain_row, shift_row, weight_row):
    return jnp.sum(layer_norm(values, gain_row, shift_row) * weight_row, -1)


def lamb_parts(weight, gradient, moment_one, moment_two, axes_list):
    mean_new = beta_first * moment_one + (1.0 - beta_first) * gradient
    square_new = beta_second * moment_two + (1.0 - beta_second) * gradient * gradient
    corrected = (
        mean_new
        / (1.0 - beta_first**STEP)
        / (jnp.sqrt(square_new / (1.0 - beta_second**STEP)) + adam_eps)
    )
    direction = corrected + decay_rate * weight
    return (
        mean_new,
        square_new,
        direction,
        jnp.sum(weight * weight, axes_list),
        jnp.sum(direction * direction, axes_list),
    )


def nn(a, b):
    return lax.dot_general(a, b, (((1,), (0,)), ((), ())), preferred_element_type=f32)


def nt(a, b):
    return lax.dot_general(a, b, (((1,), (1,)), ((), ())), preferred_element_type=f32)


def tn(a, b):
    return lax.dot_general(a, b, (((0,), (0,)), ((), ())), preferred_element_type=f32)


def encode(x_ref, w0_ref, vec_ref):
    base = nn(x_ref[...], w0_ref[0])
    normed = layer_norm(base, vec_ref[0:1], vec_ref[1:2])
    return base, normed.astype(bf16)


def local_body(x_ref, w0_ref, w1_ref, w2_ref, w3_ref, vec_ref, base_ref, a1_ref, q_ref, kv_ref):
    width = x_ref.shape[1]
    base, a1 = encode(x_ref, w0_ref, vec_ref)
    base_ref[...] = base
    a1_ref[...] = a1
    q_ref[...] = nn(a1, w1_ref[0]).astype(bf16) * jnp.asarray(scale, bf16)
    kv_ref[:, :width] = nn(a1, w2_ref[0]).astype(bf16)
    kv_ref[:, width:] = nn(a1, w3_ref[0]).astype(bf16)


def remote_body(x_ref, w0_ref, w2_ref, w3_ref, vec_ref, a1_ref, kv_ref):
    width = x_ref.shape[1]
    _, a1 = encode(x_ref, w0_ref, vec_ref)
    a1_ref[...] = a1
    kv_ref[:, :width] = nn(a1, w2_ref[0]).astype(bf16)
    kv_ref[:, width:] = nn(a1, w3_ref[0]).astype(bf16)


def project(x, weights, vectors, local):
    rows, width = x.shape
    tile = 512
    row_spec = pl.BlockSpec((tile, width), lambda i: (i, 0))
    wide_spec = pl.BlockSpec((tile, 2 * width), lambda i: (i, 0))
    used = (0, 1, 2, 3) if local else (0, 2, 3)
    weight_specs = [
        pl.BlockSpec((1, width, width), functools.partial(lambda k, i: (k, 0, 0), k)) for k in used
    ]
    outs = [jax.ShapeDtypeStruct((rows, width), bf16), jax.ShapeDtypeStruct((rows, 2 * width), bf16)]
    out_specs = [row_spec, wide_spec]
    if local:
        outs = [
            jax.ShapeDtypeStruct((rows, width), f32),
            outs[0],
            jax.ShapeDtypeStruct((rows, width), bf16),
            outs[1],
        ]
        out_specs = [row_spec, row_spec, row_spec, wide_spec]
    return pl.pallas_call(
        local_body if local else remote_body,
        grid=(rows // tile,),
        in_specs=[row_spec] + weight_specs + [pl.BlockSpec(vectors.shape, lambda i: (0, 0))],
        out_specs=out_specs,
        out_shape=outs,
        cost_estimate=pl.CostEstimate(
            flops=2 * rows * width * width * len(used),
            bytes_accessed=rows * width * 8 + len(used) * width * width * 2,
            transcendentals=rows,
        ),
        compiler_params=pltpu.CompilerParams(vmem_limit_bytes=40 << 20),
        name="project_local" if local else "project_remote",
    )(x, *([weights] * len(used)), vectors)


def split_heads(pair):
    low_half = lax.broadcasted_iota(jnp.int32, pair.shape, 1) < HD
    zero = jnp.zeros_like(pair)
    return jnp.concatenate([jnp.where(low_half, pair, zero), jnp.where(low_half, zero, pair)], 0)


def join_heads(stacked):
    half = stacked.shape[0] // 2
    upper, lower = stacked[:half], stacked[half:]
    low_half = lax.broadcasted_iota(jnp.int32, upper.shape, 1) < HD
    return jnp.where(low_half, upper, lower)


def fetch_list(block, slot, nbr_ref, own_ref, far_refs, buf, sems, listed, length):
    out = [
        pltpu.make_async_copy(own_ref.at[block], buf.at[slot, pl.ds(0, length)], sems.at[slot, 0])
    ]
    for j in range(listed):
        out.append(
            pltpu.make_async_copy(
                far_refs[j // 2].at[nbr_ref[block * listed + j]],
                buf.at[slot, pl.ds((j + 1) * length, length)],
                sems.at[slot, j + 1],
            )
        )
    return out


def forward_body(listed, slots, nbr_ref, bias_ref, q_ref, mask_ref, own_ref, r0, r1, r2, r3,
                 out_ref, lse_ref, buf, s_scr, p_scr, sems):
    block = pl.program_id(0)
    length = q_ref.shape[1]
    width = q_ref.shape[2]
    keys = (listed + 1) * length
    far = (r0, r1, r2, r3)
    fetch = functools.partial(
        fetch_list, nbr_ref=nbr_ref, own_ref=own_ref, far_refs=far, buf=buf, sems=sems,
        listed=listed, length=length,
    )

    @pl.when(block == 0)
    def _():
        for c in fetch(0, 0):
            c.start()

    @pl.when(block + 1 < slots)
    def _():
        for c in fetch(block + 1, (block + 1) % 2):
            c.start()

    slot = block % 2
    for c in fetch(block, slot):
        c.wait()
    masks = [mask_ref[block]]
    for j in range(listed):
        masks.append(mask_ref[(j // 2 + 1) * slots + nbr_ref[block * listed + j]])
    for pair in range(H // 2):
        cols = pl.ds(pair * 2 * HD, 2 * HD)
        queries = split_heads(q_ref[0, :, cols])
        s_scr[...] = nt(queries, buf[slot, :, cols])
        top = None
        for j in range(listed + 1):
            part = pl.ds(j * length, length)
            pieces = []
            for h in range(2):
                row = masks[j] + bias_ref[(block * H + pair * 2 + h) * (listed + 1) + j]
                pieces.append(s_scr[pl.ds(h * length, length), part] + row)
            piece = jnp.concatenate(pieces, 0)
            s_scr[:, part] = piece
            top = piece if top is None else jnp.maximum(top, piece)
        highest = jnp.max(top, axis=1, keepdims=True)
        mass = None
        for j in range(listed + 1):
            part = pl.ds(j * length, length)
            piece = jnp.exp(s_scr[:, part] - highest)
            s_scr[:, part] = piece
            mass = piece if mass is None else mass + piece
        total = jnp.sum(mass, axis=1, keepdims=True)
        inverse = 1.0 / total
        for j in range(listed + 1):
            part = pl.ds(j * length, length)
            p_scr[:, part] = (s_scr[:, part] * inverse).astype(bf16)
        values = buf[slot, :, pl.ds(width + pair * 2 * HD, 2 * HD)]
        out_ref[0, :, cols] = join_heads(nn(p_scr[...], values)).astype(bf16)
        lse = jnp.broadcast_to(highest + jnp.log(total), (2 * length, 128))
        lse_ref[0, :, pl.ds(pair * 2 * length, 2 * length)] = lse.T[0:1]


def attend(nbr, bias, queries, masks, own, far):
    slots, length, width = queries.shape
    listed = nbr.shape[0] // slots
    keys = (listed + 1) * length
    any_spec = pl.BlockSpec(memory_space=pl.ANY)
    return pl.pallas_call(
        functools.partial(forward_body, listed, slots),
        grid_spec=pltpu.PrefetchScalarGridSpec(
            num_scalar_prefetch=2,
            grid=(slots,),
            in_specs=[
                pl.BlockSpec((1, length, width), lambda b, *_: (b, 0, 0)),
                pl.BlockSpec(masks.shape, lambda b, *_: (0, 0, 0)),
            ]
            + [any_spec] * 5,
            out_specs=[
                pl.BlockSpec((1, length, width), lambda b, *_: (b, 0, 0)),
                pl.BlockSpec((1, 1, H * length), lambda b, *_: (b, 0, 0)),
            ],
            scratch_shapes=[
                pltpu.VMEM((2, keys, 2 * width), bf16),
                pltpu.VMEM((2 * length, keys), f32),
                pltpu.VMEM((2 * length, keys), bf16),
                pltpu.SemaphoreType.DMA((2, listed + 1)),
            ],
        ),
        out_shape=[
            jax.ShapeDtypeStruct((slots, length, width), bf16),
            jax.ShapeDtypeStruct((slots, 1, H * length), f32),
        ],
        cost_estimate=pl.CostEstimate(
            flops=4 * slots * length * keys * width * 2,
            bytes_accessed=slots * keys * width * 4,
            transcendentals=slots * length * keys * H,
        ),
        compiler_params=pltpu.CompilerParams(vmem_limit_bytes=40 << 20),
        name="attention_forward",
    )(nbr, bias, queries, masks, own, *far)


def backward_body(listed, slots, nbr_ref, bias_ref, q_ref, g_ref, lse_ref, mask_ref, own_ref,
                  r0, r1, r2, r3, dq_ref, down_ref, dfar_ref, dbias_ref,
                  buf, mcol, p_scr, g_scr, pl_scr, ds_scr, acc, sems, msems):
    step = pl.program_id(0)
    length = q_ref.shape[1]
    width = q_ref.shape[2]
    far = (r0, r1, r2, r3)
    fetch = functools.partial(
        fetch_list, nbr_ref=nbr_ref, own_ref=own_ref, far_refs=far, buf=buf, sems=sems,
        listed=listed, length=length,
    )

    def mask_list(block, slot):
        out = [
            pltpu.make_async_copy(
                mask_ref.at[block], mcol.at[slot, pl.ds(0, length)], msems.at[slot, 0]
            )
        ]
        for j in range(listed):
            out.append(
                pltpu.make_async_copy(
                    mask_ref.at[(j // 2 + 1) * slots + nbr_ref[block * listed + j]],
                    mcol.at[slot, pl.ds((j + 1) * length, length)],
                    msems.at[slot, j + 1],
                )
            )
        return out

    @pl.when(step == 0)
    def _():
        for c in fetch(0, 0) + mask_list(0, 0):
            c.start()
        for i in range(4 * slots):
            acc[i] = jnp.zeros(acc.shape[1:], f32)

    @pl.when(step + 1 < slots)
    def _():
        for c in fetch(step + 1, (step + 1) % 2) + mask_list(step + 1, (step + 1) % 2):
            c.start()

    @pl.when(step < slots)
    def _():
        block = step
        slot = block % 2
        for c in fetch(block, slot) + mask_list(block, slot):
            c.wait()
        left = lax.broadcasted_iota(jnp.int32, (1, 2 * length), 1) < length
        for pair in range(H // 2):
            cols = pl.ds(pair * 2 * HD, 2 * HD)
            vcols = pl.ds(width + pair * 2 * HD, 2 * HD)
            rows = pl.ds(pair * 2 * length, 2 * length)
            queries = split_heads(q_ref[0, :, cols])
            grads = split_heads(g_ref[0, :, cols])
            lse = lse_ref[0, :, rows]
            p_scr[...] = nt(buf[slot, :, cols], queries)
            g_scr[...] = nt(buf[slot, :, vcols], grads)
            inner = None
            for j in range(listed + 1):
                part = pl.ds(j * length, length)
                at = (block * H + pair * 2) * (listed + 1) + j
                row = jnp.where(left, bias_ref[at], bias_ref[at + listed + 1]) - lse
                mask = mcol[slot, part]
                mask = jnp.concatenate([mask, mask], 1)
                probs = jnp.exp(p_scr[part] + row + mask)
                p_scr[part] = probs
                pl_scr[part] = probs.astype(bf16)
                term = jnp.sum(probs * g_scr[part], axis=0, keepdims=True)
                inner = term if inner is None else inner + term
            for j in range(listed + 1):
                part = pl.ds(j * length, length)
                ds = p_scr[part] * (g_scr[part] - inner)
                ds_scr[part] = ds.astype(bf16)
                dbias_ref[0, pl.ds(j, 1), rows] = jnp.sum(ds, axis=0, keepdims=True)
            dq = tn(ds_scr[...], buf[slot, :, cols])
            dq_ref[0, :, cols] = (join_heads(dq) * scale).astype(bf16)
            dk = nn(ds_scr[...], queries)
            dv = nn(pl_scr[...], grads)
            down_ref[0, :, cols] = dk[:length].astype(bf16)
            down_ref[0, :, vcols] = dv[:length].astype(bf16)
            for j in range(listed):
                at = (j // 2) * slots + nbr_ref[block * listed + j]
                acc[at, :, cols] += dk[(j + 1) * length : (j + 2) * length]
                acc[at, :, vcols] += dv[(j + 1) * length : (j + 2) * length]

    @pl.when(step >= slots)
    def _():
        for o in range(4):
            dfar_ref[o, 0] = acc[o * slots + step - slots].astype(bf16)


def attend_back(nbr, bias, queries, grads, lse, mask_cols, own, far):
    slots, length, width = queries.shape
    listed = nbr.shape[0] // slots
    keys = (listed + 1) * length
    any_spec = pl.BlockSpec(memory_space=pl.ANY)
    here = lambda b, *_: (jnp.minimum(b, slots - 1), 0, 0)
    return pl.pallas_call(
        functools.partial(backward_body, listed, slots),
        grid_spec=pltpu.PrefetchScalarGridSpec(
            num_scalar_prefetch=2,
            grid=(2 * slots,),
            in_specs=[
                pl.BlockSpec((1, length, width), here),
                pl.BlockSpec((1, length, width), here),
                pl.BlockSpec((1, 1, H * length), here),
            ]
            + [any_spec] * 6,
            out_specs=[
                pl.BlockSpec((1, length, width), here),
                pl.BlockSpec((1, length, 2 * width), here),
                pl.BlockSpec(
                    (4, 1, length, 2 * width), lambda b, *_: (0, jnp.maximum(b - slots, 0), 0, 0)
                ),
                pl.BlockSpec((1, listed + 1, H * length), here),
            ],
            scratch_shapes=[
                pltpu.VMEM((2, keys, 2 * width), bf16),
                pltpu.VMEM((2, keys, length), f32),
                pltpu.VMEM((keys, 2 * length), f32),
                pltpu.VMEM((keys, 2 * length), f32),
                pltpu.VMEM((keys, 2 * length), bf16),
                pltpu.VMEM((keys, 2 * length), bf16),
                pltpu.VMEM((4 * slots, length, 2 * width), f32),
                pltpu.SemaphoreType.DMA((2, listed + 1)),
                pltpu.SemaphoreType.DMA((2, listed + 1)),
            ],
        ),
        out_shape=[
            jax.ShapeDtypeStruct((slots, length, width), bf16),
            jax.ShapeDtypeStruct((slots, length, 2 * width), bf16),
            jax.ShapeDtypeStruct((4, slots, length, 2 * width), bf16),
            jax.ShapeDtypeStruct((slots, listed + 1, H * length), f32),
        ],
        cost_estimate=pl.CostEstimate(
            flops=10 * slots * length * keys * width * 2,
            bytes_accessed=slots * keys * width * 4,
            transcendentals=slots * length * keys * H,
        ),
        compiler_params=pltpu.CompilerParams(vmem_limit_bytes=60 << 20),
        name="attention_backward",
    )(nbr, bias, queries, grads, lse, mask_cols, own, *far)


def halved(value, order):
    count = value.shape[0]
    bits = count.bit_length() - 1
    place = lax.axis_index(both)
    value = value.reshape((2,) * bits + value.shape[1:])
    left = list(range(bits - 1, -1, -1))
    for bit in order:
        axis = left.index(bit)
        left.pop(axis)
        mine = (place >> bit) & 1
        keep = lax.dynamic_index_in_dim(value, mine, axis, keepdims=False)
        send = lax.dynamic_index_in_dim(value, 1 - mine, axis, keepdims=False)
        got = lax.ppermute(send, both, [(i, i ^ (1 << bit)) for i in range(count)])
        value = keep + got
    return value


def bit_orders(count):
    bits = list(range(count.bit_length() - 1))
    rest = bits[1:]
    orders = []
    for turn in range(4):
        k = turn % len(rest)
        orders.append(bits[:1] + rest[k:] + rest[:k])
    return orders


def per_device(
    features,
    targets,
    node_mask,
    block_counts,
    neighbours,
    edge_types,
    proj_weights,
    ffn_weights,
    vector_params,
    proj_mean,
    ffn_mean,
    vector_mean,
    proj_square,
    ffn_square,
    vector_square,
):
    span_count = lax.axis_size("nodes")
    pair_count = lax.axis_size("fsdp")
    device_count = span_count * pair_count
    slot_count, listed = neighbours.shape
    row_count, model_width = features.shape
    block_len = row_count // slot_count
    shard = proj_weights.shape[1]
    shifts = (1, -1, span_count // 4, span_count // 2)

    far_features = [passed_along(features, s) for s in shifts]

    live_slots = (jnp.arange(slot_count) < block_counts[0]).astype(f32)
    valid_nodes = node_mask.astype(f32).reshape(slot_count, block_len) * live_slots[:, None]
    valid_rows = valid_nodes.reshape(row_count)

    mask_rows = row_count // model_width
    used_rows = 5 * shard + 1 + mask_rows
    packed = jnp.concatenate(
        [
            proj_weights.astype(bf16).reshape(5 * shard, model_width),
            jnp.pad(vector_params.astype(bf16).reshape(1, 8 * shard), ((0, 0), (0, model_width - 8 * shard))),
            valid_rows.astype(bf16).reshape(mask_rows, model_width),
            jnp.zeros((-used_rows % 16, model_width), bf16),
        ],
        0,
    )
    gathered = lax.all_gather(packed, both, axis=0, tiled=False)
    low_ffn = lax.all_gather(ffn_weights.astype(bf16), both, axis=1, tiled=True)
    low_proj = (
        gathered[:, : 5 * shard]
        .reshape(device_count, 5, shard, model_width)
        .transpose(1, 0, 2, 3)
        .reshape(5, model_width, model_width)
    )
    low_vector = (
        gathered[:, 5 * shard, : 8 * shard]
        .reshape(device_count, 8, shard)
        .transpose(1, 0, 2)
        .reshape(8, model_width)
    )
    all_valid = gathered[:, 5 * shard + 1 : used_rows].astype(f32)
    node_total = jnp.sum(all_valid)
    gain_rows = low_vector.astype(f32)

    rank = lax.axis_index("nodes")
    pair = lax.axis_index("fsdp")
    all_valid = all_valid.reshape(device_count, slot_count, block_len)
    far_valid = [
        lax.dynamic_index_in_dim(
            all_valid, ((rank - s) % span_count) * pair_count + pair, 0, keepdims=False
        )
        for s in shifts
    ]
    key_masks = (jnp.concatenate([valid_nodes] + far_valid, 0) - 1.0) * mask_fill
    mask_lines = key_masks[:, None, :]
    mask_cols = jnp.broadcast_to(key_masks[:, :, None], key_masks.shape + (block_len,))

    type_table = gain_rows[7].reshape(NTYPES, H)
    type_onehot = (
        edge_types[:, :, None] == jnp.arange(NTYPES, dtype=jnp.int32)[None, None, :]
    ).astype(f32)
    pair_bias = jnp.einsum("sjt,th->shj", type_onehot, type_table, precision=precise).reshape(-1)
    flat_nbr = neighbours.reshape(-1)

    base, attn_in, queries, own_kv = project(features, low_proj, gain_rows, True)
    far_a1 = []
    far_kv = []
    for piece in far_features:
        a1, kv = project(piece, low_proj, gain_rows, False)
        far_a1.append(a1)
        far_kv.append(kv.reshape(slot_count, block_len, 2 * model_width))
    own_blocks = own_kv.reshape(slot_count, block_len, 2 * model_width)
    query_blocks = queries.reshape(slot_count, block_len, model_width)

    attn_out, lse = attend(flat_nbr, pair_bias, query_blocks, mask_lines, own_blocks, far_kv)
    attn_rows = attn_out.reshape(row_count, model_width)
    attn_y = nn(attn_rows, low_proj[4])
    middle = base + attn_y
    normed_two, norm_two_back = jax.vjp(layer_norm, middle, gain_rows[2], gain_rows[3])
    ffn_in = normed_two.astype(bf16)
    hidden_pre = nn(ffn_in, low_ffn[0])
    hidden_act, gelu_back = jax.vjp(jax.nn.gelu, hidden_pre)
    hidden = hidden_act.astype(bf16)
    ffn_y = nt(hidden, low_ffn[1])
    final = middle + ffn_y
    predict, head_back = jax.vjp(head_out, final, gain_rows[4], gain_rows[5], gain_rows[6])
    error = predict - targets
    local_sums = jnp.stack(
        [jnp.sum(valid_rows * error * error)]
        + [jnp.sum(valid_rows[:, None] * piece * piece) for piece in (middle, attn_y, final, ffn_y)]
    )

    grad_pred = 2.0 * valid_rows * error / node_total
    grad_final, grad_gain_f, grad_shift_f, grad_head = head_back(grad_pred)
    grad_ffn_y = grad_final.astype(bf16)
    grad_down = tn(grad_ffn_y, hidden)
    grad_hidden = nn(grad_ffn_y, low_ffn[1])
    grad_pre = gelu_back(grad_hidden)[0].astype(bf16)
    grad_up = tn(ffn_in, grad_pre)
    shard_ffn = lax.psum_scatter(
        jnp.stack([grad_up, grad_down]), both, scatter_dimension=1, tiled=True
    )
    grad_ffn_in = nt(grad_pre, low_ffn[0])
    grad_mid_norm, grad_gain_two, grad_shift_two = norm_two_back(grad_ffn_in)
    grad_middle = grad_final + grad_mid_norm
    grad_attn_y = grad_middle.astype(bf16)
    grad_out_proj = tn(attn_rows, grad_attn_y)
    grad_attn = nt(grad_attn_y, low_proj[4]).astype(bf16).reshape(query_blocks.shape)

    grad_q, grad_own, grad_far, grad_bias = attend_back(
        flat_nbr, pair_bias, query_blocks, grad_attn, lse, mask_cols, own_blocks, far_kv
    )
    grad_q = grad_q.reshape(row_count, model_width)
    grad_own = grad_own.reshape(row_count, 2 * model_width)
    low_kv = jnp.concatenate([low_proj[2], low_proj[3]], 1)
    back_pieces = []
    for index, shift_by in reversed(list(enumerate(shifts))):
        piece = grad_far[index].reshape(row_count, 2 * model_width)
        back_pieces.append(passed_along(nt(piece, low_kv).astype(bf16), -shift_by))
    grad_query_w = tn(attn_in, grad_q)
    grad_kv_w = tn(attn_in, grad_own)
    for index in range(4):
        grad_kv_w = grad_kv_w + tn(far_a1[index], grad_far[index].reshape(row_count, 2 * model_width))
    early = jnp.stack(
        [grad_query_w, grad_kv_w[:, :model_width], grad_kv_w[:, model_width:], grad_out_proj]
    )
    early = early.reshape(4, device_count, shard, model_width)
    shard_early = [
        halved(early[index], order) for index, order in enumerate(bit_orders(device_count))
    ]
    grad_attn_in = nt(grad_q, low_proj[1]) + nt(grad_own, low_kv)
    for piece in back_pieces:
        grad_attn_in = grad_attn_in + piece.astype(f32)
    _, norm_one_back = jax.vjp(layer_norm, base, gain_rows[0], gain_rows[1])
    grad_base_norm, grad_gain_one, grad_shift_one = norm_one_back(grad_attn_in)
    grad_base = (grad_middle + grad_base_norm).astype(bf16)
    grad_encoder = tn(features, grad_base)
    bias_sums = jnp.sum(grad_bias.reshape(slot_count, listed + 1, H, block_len), -1)
    grad_table = jnp.einsum("sjt,sjh->th", type_onehot, bias_sums, precision=precise)
    grad_vector_all = jnp.stack(
        [
            grad_gain_one,
            grad_shift_one,
            grad_gain_two,
            grad_shift_two,
            grad_gain_f,
            grad_shift_f,
            grad_head,
            grad_table.reshape(model_width),
        ]
    )
    vector_lines = (
        grad_vector_all.reshape(8, device_count, shard)
        .transpose(1, 0, 2)
        .reshape(device_count, 1, 8 * shard)
    )
    vector_lines = jnp.pad(vector_lines, ((0, 0), (0, 0), (0, model_width - 8 * shard)))
    late = jnp.concatenate(
        [grad_encoder.reshape(device_count, shard, model_width), vector_lines], 1
    )
    late = halved(late, list(range(device_count.bit_length() - 1)))
    shard_proj = jnp.stack([late[:shard]] + shard_early)
    shard_vector = late[shard, : 8 * shard].reshape(8, shard)

    proj_parts = lamb_parts(proj_weights, shard_proj, proj_mean, proj_square, (1, 2))
    ffn_parts = lamb_parts(ffn_weights, shard_ffn, ffn_mean, ffn_square, (1, 2))
    vector_parts = lamb_parts(vector_params, shard_vector, vector_mean, vector_square, (1,))
    mine = jnp.concatenate(
        [
            proj_parts[3], ffn_parts[3], vector_parts[3],
            proj_parts[4], ffn_parts[4], vector_parts[4],
            local_sums,
        ]
    )
    mine = jnp.pad(mine, (0, 128 - mine.shape[0]))
    everyone = lax.all_to_all(
        jnp.broadcast_to(mine[None], (device_count, 128)), both, 0, 0, tiled=True
    )
    sums = jnp.sum(everyone, 0)
    norm_pairs = jnp.sqrt(jnp.stack([sums[:15], sums[15:30]], 1))
    stat_sums = sums[30:35]
    ratio = norm_pairs[:, 0] / norm_pairs[:, 1]
    updated_proj = proj_weights - learn_rate * ratio[0:5, None, None] * proj_parts[2]
    updated_ffn = ffn_weights - learn_rate * ratio[5:7, None, None] * ffn_parts[2]
    updated_vector = vector_params - learn_rate * ratio[7:15, None] * vector_parts[2]
    train_loss = stat_sums[0] / node_total
    stream_scale = jnp.sqrt(stat_sums[1:] / (node_total * model_width))
    return (
        updated_proj,
        updated_ffn,
        updated_vector,
        proj_parts[0],
        ffn_parts[0],
        vector_parts[0],
        proj_parts[1],
        ffn_parts[1],
        vector_parts[1],
        updated_proj.astype(bf16),
        updated_ffn.astype(bf16),
        updated_vector.astype(bf16),
        norm_pairs,
        stream_scale,
        train_loss,
    )


def solution(mesh):
    rows = P(("nodes", "fsdp"), None)
    line = P(("nodes", "fsdp"))
    cube = P(None, ("nodes", "fsdp"), None)
    flat = P(None, ("nodes", "fsdp"))
    state = (cube, cube, flat)
    return jax.shard_map(
        per_device,
        mesh=mesh,
        in_specs=(rows, line, line, line, rows, rows) + state * 3,
        out_specs=state * 4 + (P(), P(), P()),
        check_vma=False,
    )
```

```python
import functools
import jax
import jax.numpy as jnp
from jax import lax
from jax.experimental import pallas as pl
from jax.experimental.pallas import tpu as pltpu
from jax.sharding import PartitionSpec as P

H = 8
HD = 64
STEP = 10
NTYPES = 64

norm_eps = 1e-05
adam_eps = 1e-06
beta_first = 0.9
beta_second = 0.999
decay_rate = 0.01
learn_rate = 0.2
mask_fill = 1000000000.0
precise = lax.Precision.HIGHEST
both = ("nodes", "fsdp")
f32 = jnp.float32
bf16 = jnp.bfloat16
scale = HD ** (-0.5)


def passed_along(value, steps):
    count = lax.axis_size("nodes")
    pairs = [(source, (source + steps) % count) for source in range(count)]
    return lax.ppermute(value, "nodes", pairs)


def layer_norm(values, gain_row, shift_row):
    center = values - jnp.mean(values, -1, keepdims=True)
    spread = jnp.mean(center * center, -1, keepdims=True)
    return center * lax.rsqrt(spread + norm_eps) * gain_row + shift_row


def head_out(values, gain_row, shift_row, weight_row):
    return jnp.sum(layer_norm(values, gain_row, shift_row) * weight_row, -1)


def lamb_parts(weight, gradient, moment_one, moment_two, axes_list):
    mean_new = beta_first * moment_one + (1.0 - beta_first) * gradient
    square_new = beta_second * moment_two + (1.0 - beta_second) * gradient * gradient
    corrected = (
        mean_new
        / (1.0 - beta_first**STEP)
        / (jnp.sqrt(square_new / (1.0 - beta_second**STEP)) + adam_eps)
    )
    direction = corrected + decay_rate * weight
    return (
        mean_new,
        square_new,
        direction,
        jnp.sum(weight * weight, axes_list),
        jnp.sum(direction * direction, axes_list),
    )


def nn(a, b):
    return lax.dot_general(a, b, (((1,), (0,)), ((), ())), preferred_element_type=f32)


def nt(a, b):
    return lax.dot_general(a, b, (((1,), (1,)), ((), ())), preferred_element_type=f32)


def tn(a, b):
    return lax.dot_general(a, b, (((0,), (0,)), ((), ())), preferred_element_type=f32)


def encode(x_ref, w0_ref, vec_ref):
    base = nn(x_ref[...], w0_ref[0])
    normed = layer_norm(base, vec_ref[0:1], vec_ref[1:2])
    return base, normed.astype(bf16)


def local_body(x_ref, w0_ref, w1_ref, w2_ref, w3_ref, vec_ref, base_ref, a1_ref, q_ref, kv_ref):
    width = x_ref.shape[1]
    base, a1 = encode(x_ref, w0_ref, vec_ref)
    base_ref[...] = base
    a1_ref[...] = a1
    q_ref[...] = nn(a1, w1_ref[0]).astype(bf16) * jnp.asarray(scale, bf16)
    kv_ref[:, :width] = nn(a1, w2_ref[0]).astype(bf16)
    kv_ref[:, width:] = nn(a1, w3_ref[0]).astype(bf16)


def remote_body(x_ref, w0_ref, w2_ref, w3_ref, vec_ref, a1_ref, kv_ref):
    width = x_ref.shape[1]
    _, a1 = encode(x_ref, w0_ref, vec_ref)
    a1_ref[...] = a1
    kv_ref[:, :width] = nn(a1, w2_ref[0]).astype(bf16)
    kv_ref[:, width:] = nn(a1, w3_ref[0]).astype(bf16)


def project(x, weights, vectors, local):
    rows, width = x.shape
    tile = 512
    row_spec = pl.BlockSpec((tile, width), lambda i: (i, 0))
    wide_spec = pl.BlockSpec((tile, 2 * width), lambda i: (i, 0))
    used = (0, 1, 2, 3) if local else (0, 2, 3)
    weight_specs = [
        pl.BlockSpec((1, width, width), functools.partial(lambda k, i: (k, 0, 0), k)) for k in used
    ]
    outs = [jax.ShapeDtypeStruct((rows, width), bf16), jax.ShapeDtypeStruct((rows, 2 * width), bf16)]
    out_specs = [row_spec, wide_spec]
    if local:
        outs = [
            jax.ShapeDtypeStruct((rows, width), f32),
            outs[0],
            jax.ShapeDtypeStruct((rows, width), bf16),
            outs[1],
        ]
        out_specs = [row_spec, row_spec, row_spec, wide_spec]
    return pl.pallas_call(
        local_body if local else remote_body,
        grid=(rows // tile,),
        in_specs=[row_spec] + weight_specs + [pl.BlockSpec(vectors.shape, lambda i: (0, 0))],
        out_specs=out_specs,
        out_shape=outs,
        cost_estimate=pl.CostEstimate(
            flops=2 * rows * width * width * len(used),
            bytes_accessed=rows * width * 8 + len(used) * width * width * 2,
            transcendentals=rows,
        ),
        compiler_params=pltpu.CompilerParams(vmem_limit_bytes=40 << 20),
        name="project_local" if local else "project_remote",
    )(x, *([weights] * len(used)), vectors)


def split_heads(pair):
    low_half = lax.broadcasted_iota(jnp.int32, pair.shape, 1) < HD
    zero = jnp.zeros_like(pair)
    return jnp.concatenate([jnp.where(low_half, pair, zero), jnp.where(low_half, zero, pair)], 0)


def join_heads(stacked):
    half = stacked.shape[0] // 2
    upper, lower = stacked[:half], stacked[half:]
    low_half = lax.broadcasted_iota(jnp.int32, upper.shape, 1) < HD
    return jnp.where(low_half, upper, lower)


def fetch_list(block, slot, nbr_ref, own_ref, far_refs, buf, sems, listed, length):
    out = [
        pltpu.make_async_copy(own_ref.at[block], buf.at[slot, pl.ds(0, length)], sems.at[slot, 0])
    ]
    for j in range(listed):
        out.append(
            pltpu.make_async_copy(
                far_refs[j // 2].at[nbr_ref[block * listed + j]],
                buf.at[slot, pl.ds((j + 1) * length, length)],
                sems.at[slot, j + 1],
            )
        )
    return out


def forward_body(listed, slots, nbr_ref, bias_ref, q_ref, mask_ref, own_ref, r0, r1, r2, r3,
                 out_ref, lse_ref, buf, s_scr, p_scr, sems):
    block = pl.program_id(0)
    length = q_ref.shape[1]
    width = q_ref.shape[2]
    far = (r0, r1, r2, r3)
    fetch = functools.partial(
        fetch_list, nbr_ref=nbr_ref, own_ref=own_ref, far_refs=far, buf=buf, sems=sems,
        listed=listed, length=length,
    )

    @pl.when(block == 0)
    def _():
        for c in fetch(0, 0):
            c.start()

    @pl.when(block + 1 < slots)
    def _():
        for c in fetch(block + 1, (block + 1) % 2):
            c.start()

    slot = block % 2
    for c in fetch(block, slot):
        c.wait()
    masks = [mask_ref[block]]
    for j in range(listed):
        masks.append(mask_ref[(j // 2 + 1) * slots + nbr_ref[block * listed + j]])
    for pair in range(H // 2):
        cols = pl.ds(pair * 2 * HD, 2 * HD)
        queries = split_heads(q_ref[0, :, cols])
        s_scr[...] = nt(queries, buf[slot, :, cols])
        top = None
        for j in range(listed + 1):
            part = pl.ds(j * length, length)
            pieces = []
            for h in range(2):
                row = masks[j] + bias_ref[(block * H + pair * 2 + h) * (listed + 1) + j]
                pieces.append(s_scr[pl.ds(h * length, length), part] + row)
            piece = jnp.concatenate(pieces, 0)
            s_scr[:, part] = piece
            top = piece if top is None else jnp.maximum(top, piece)
        highest = jnp.max(top, axis=1, keepdims=True)
        mass = None
        for j in range(listed + 1):
            part = pl.ds(j * length, length)
            piece = jnp.exp(s_scr[:, part] - highest)
            s_scr[:, part] = piece
            mass = piece if mass is None else mass + piece
        total = jnp.sum(mass, axis=1, keepdims=True)
        inverse = 1.0 / total
        for j in range(listed + 1):
            part = pl.ds(j * length, length)
            p_scr[:, part] = (s_scr[:, part] * inverse).astype(bf16)
        values = buf[slot, :, pl.ds(width + pair * 2 * HD, 2 * HD)]
        out_ref[0, :, cols] = join_heads(nn(p_scr[...], values)).astype(bf16)
        lse = jnp.broadcast_to(highest + jnp.log(total), (2 * length, 128))
        lse_ref[0, :, pl.ds(pair * 2 * length, 2 * length)] = lse.T[0:1]


def attend(nbr, bias, queries, masks, own, far):
    slots, length, width = queries.shape
    listed = nbr.shape[0] // slots
    keys = (listed + 1) * length
    any_spec = pl.BlockSpec(memory_space=pl.ANY)
    return pl.pallas_call(
        functools.partial(forward_body, listed, slots),
        grid_spec=pltpu.PrefetchScalarGridSpec(
            num_scalar_prefetch=2,
            grid=(slots,),
            in_specs=[
                pl.BlockSpec((1, length, width), lambda b, *_: (b, 0, 0)),
                pl.BlockSpec(masks.shape, lambda b, *_: (0, 0, 0)),
            ]
            + [any_spec] * 5,
            out_specs=[
                pl.BlockSpec((1, length, width), lambda b, *_: (b, 0, 0)),
                pl.BlockSpec((1, 1, H * length), lambda b, *_: (b, 0, 0)),
            ],
            scratch_shapes=[
                pltpu.VMEM((2, keys, 2 * width), bf16),
                pltpu.VMEM((2 * length, keys), f32),
                pltpu.VMEM((2 * length, keys), bf16),
                pltpu.SemaphoreType.DMA((2, listed + 1)),
            ],
        ),
        out_shape=[
            jax.ShapeDtypeStruct((slots, length, width), bf16),
            jax.ShapeDtypeStruct((slots, 1, H * length), f32),
        ],
        cost_estimate=pl.CostEstimate(
            flops=4 * slots * length * keys * width * 2,
            bytes_accessed=slots * keys * width * 4,
            transcendentals=slots * length * keys * H,
        ),
        compiler_params=pltpu.CompilerParams(vmem_limit_bytes=40 << 20),
        name="attention_forward",
    )(nbr, bias, queries, masks, own, *far)


def backward_body(listed, slots, own, first, count, nbr_ref, bias_ref, q_ref, g_ref, lse_ref,
                  inner_ref, mask_ref, *refs):
    refs = list(refs)
    own_ref = refs.pop(0) if own else None
    prev_ref = refs.pop(0) if own else None
    far = [refs.pop(0) for _ in range(count // 2)]
    dq_ref = refs.pop(0)
    down_ref = refs.pop(0) if own else None
    dfar_ref, dbias_ref, buf, mcol, p_scr, g_scr, pl_scr, ds_scr, acc, sems, msems = refs
    step = pl.program_id(0)
    length = q_ref.shape[1]
    width = q_ref.shape[2]
    lead = 1 if own else 0
    blocks = count + lead

    def fetch(block, slot):
        out = []
        for i in range(blocks):
            part = pl.ds(i * length, length)
            if i < lead:
                source, mask_at = own_ref.at[block], block
            else:
                j = first + i - lead
                at = nbr_ref[block * listed + j]
                source, mask_at = far[(i - lead) // 2].at[at], (j // 2 + 1) * slots + at
            out.append(pltpu.make_async_copy(source, buf.at[slot, part], sems.at[slot, i]))
            out.append(
                pltpu.make_async_copy(mask_ref.at[mask_at], mcol.at[slot, part], msems.at[slot, i])
            )
        return out

    @pl.when(step == 0)
    def _():
        for c in fetch(0, 0):
            c.start()
        for i in range(acc.shape[0]):
            acc[i] = jnp.zeros(acc.shape[1:], f32)

    @pl.when(step + 1 < slots)
    def _():
        for c in fetch(step + 1, (step + 1) % 2):
            c.start()

    @pl.when(step < slots)
    def _():
        block = step
        slot = block % 2
        for c in fetch(block, slot):
            c.wait()
        left = lax.broadcasted_iota(jnp.int32, (1, 2 * length), 1) < length
        for pair in range(H // 2):
            cols = pl.ds(pair * 2 * HD, 2 * HD)
            vcols = pl.ds(width + pair * 2 * HD, 2 * HD)
            rows = pl.ds(pair * 2 * length, 2 * length)
            queries = split_heads(q_ref[0, :, cols])
            grads = split_heads(g_ref[0, :, cols])
            lse = lse_ref[0, :, rows]
            inner = inner_ref[0, :, rows]
            p_scr[...] = nt(buf[slot, :, cols], queries)
            g_scr[...] = nt(buf[slot, :, vcols], grads)
            for i in range(blocks):
                part = pl.ds(i * length, length)
                j = i if own else first + 1 + i
                at = (block * H + pair * 2) * (listed + 1) + j
                row = jnp.where(left, bias_ref[at], bias_ref[at + listed + 1]) - lse
                mask = mcol[slot, part]
                mask = jnp.concatenate([mask, mask], 1)
                probs = jnp.exp(p_scr[part] + row + mask)
                pl_scr[part] = probs.astype(bf16)
                ds = probs * (g_scr[part] - inner)
                ds_scr[part] = ds.astype(bf16)
                dbias_ref[0, pl.ds(i, 1), rows] = jnp.sum(ds, axis=0, keepdims=True)
            dq = join_heads(tn(ds_scr[...], buf[slot, :, cols])) * scale
            if own:
                dq_ref[0, :, cols] = (dq + prev_ref[0, :, cols]).astype(bf16)
            else:
                dq_ref[0, :, cols] = dq
            dk = nn(ds_scr[...], queries)
            dv = nn(pl_scr[...], grads)
            if own:
                down_ref[0, :, cols] = dk[:length].astype(bf16)
                down_ref[0, :, vcols] = dv[:length].astype(bf16)
            for i in range(count):
                part = slice((i + lead) * length, (i + lead + 1) * length)
                at = (i // 2) * slots + nbr_ref[block * listed + first + i]
                acc[at, :, cols] += dk[part]
                acc[at, :, vcols] += dv[part]

    @pl.when(step >= slots)
    def _():
        for o in range(count // 2):
            dfar_ref[o, 0] = acc[o * slots + step - slots].astype(bf16)


def attend_back(nbr, bias, queries, grads, lse, inner, mask_cols, own, before, far, first):
    slots, length, width = queries.shape
    listed = nbr.shape[0] // slots
    lead = 0 if own is None else 1
    count = 2 * len(far)
    keys = (count + lead) * length
    any_spec = pl.BlockSpec(memory_space=pl.ANY)
    here = lambda b, *_: (jnp.minimum(b, slots - 1), 0, 0)
    block_spec = pl.BlockSpec((1, length, width), here)
    line_spec = pl.BlockSpec((1, 1, H * length), here)
    outs = [jax.ShapeDtypeStruct((slots, length, width), bf16 if lead else f32)]
    out_specs = [block_spec]
    if lead:
        outs.append(jax.ShapeDtypeStruct((slots, length, 2 * width), bf16))
        out_specs.append(pl.BlockSpec((1, length, 2 * width), here))
    outs += [
        jax.ShapeDtypeStruct((len(far), slots, length, 2 * width), bf16),
        jax.ShapeDtypeStruct((slots, count + lead, H * length), f32),
    ]
    out_specs += [
        pl.BlockSpec(
            (len(far), 1, length, 2 * width), lambda b, *_: (0, jnp.maximum(b - slots, 0), 0, 0)
        ),
        pl.BlockSpec((1, count + lead, H * length), here),
    ]
    return pl.pallas_call(
        functools.partial(backward_body, listed, slots, bool(lead), first, count),
        grid_spec=pltpu.PrefetchScalarGridSpec(
            num_scalar_prefetch=2,
            grid=(2 * slots,),
            in_specs=[block_spec, block_spec, line_spec, line_spec, any_spec]
            + [any_spec, block_spec] * lead
            + [any_spec] * len(far),
            out_specs=out_specs,
            scratch_shapes=[
                pltpu.VMEM((2, keys, 2 * width), bf16),
                pltpu.VMEM((2, keys, length), f32),
                pltpu.VMEM((keys, 2 * length), f32),
                pltpu.VMEM((keys, 2 * length), f32),
                pltpu.VMEM((keys, 2 * length), bf16),
                pltpu.VMEM((keys, 2 * length), bf16),
                pltpu.VMEM((len(far) * slots, length, 2 * width), f32),
                pltpu.SemaphoreType.DMA((2, count + lead)),
                pltpu.SemaphoreType.DMA((2, count + lead)),
            ],
        ),
        out_shape=outs,
        cost_estimate=pl.CostEstimate(
            flops=20 * slots * length * keys * width * 2,
            bytes_accessed=slots * keys * width * 4,
            transcendentals=slots * length * keys * H,
        ),
        compiler_params=pltpu.CompilerParams(vmem_limit_bytes=48 << 20),
        name="attention_backward_near" if lead else "attention_backward_far",
    )(nbr, bias, queries, grads, lse, inner, mask_cols, *([own, before] if lead else []), *far)


def swap(value, bit):
    count = lax.axis_size("nodes") * lax.axis_size("fsdp")
    return lax.ppermute(value, both, [(i, i ^ (1 << bit)) for i in range(count)])


def halved(value, order):
    bits = value.shape[0].bit_length() - 1
    place = lax.axis_index(both)
    value = value.reshape((2,) * bits + value.shape[1:])
    left = list(range(bits - 1, -1, -1))
    for bit in order:
        axis = left.index(bit)
        left.pop(axis)
        mine = (place >> bit) & 1
        keep = lax.dynamic_index_in_dim(value, mine, axis, keepdims=False)
        send = lax.dynamic_index_in_dim(value, 1 - mine, axis, keepdims=False)
        got = swap(send, bit)
        value = keep + got
    return value


def doubled(value, bits):
    place = lax.axis_index(both)
    for turn, bit in enumerate(range(bits - 1, -1, -1)):
        got = swap(value, bit)
        mine = (place >> bit) & 1
        value = jnp.where(
            mine == 0, jnp.stack([value, got], turn), jnp.stack([got, value], turn)
        )
    return value.reshape((1 << bits,) + value.shape[bits:])


def orders_of(bits):
    rest = list(range(3, bits))
    return ([0, 1, 2] + rest, [0, 2, 1] + rest)


def per_device(
    features,
    targets,
    node_mask,
    block_counts,
    neighbours,
    edge_types,
    proj_weights,
    ffn_weights,
    vector_params,
    proj_mean,
    ffn_mean,
    vector_mean,
    proj_square,
    ffn_square,
    vector_square,
):
    span_count = lax.axis_size("nodes")
    pair_count = lax.axis_size("fsdp")
    device_count = span_count * pair_count
    slot_count, listed = neighbours.shape
    row_count, model_width = features.shape
    block_len = row_count // slot_count
    shard = proj_weights.shape[1]
    shifts = (1, -1, span_count // 4, span_count // 2)

    bits = device_count.bit_length() - 1
    far_features = [None] * 4
    for index in (3, 2):
        far_features[index] = passed_along(features, shifts[index])

    live_slots = (jnp.arange(slot_count) < block_counts[0]).astype(f32)
    valid_nodes = node_mask.astype(f32).reshape(slot_count, block_len) * live_slots[:, None]
    valid_rows = valid_nodes.reshape(row_count)

    mask_rows = row_count // model_width
    used_rows = 5 * shard + 1 + mask_rows
    packed = jnp.concatenate(
        [
            proj_weights.astype(bf16).reshape(5 * shard, model_width),
            jnp.pad(vector_params.astype(bf16).reshape(1, 8 * shard), ((0, 0), (0, model_width - 8 * shard))),
            valid_rows.astype(bf16).reshape(mask_rows, model_width),
            jnp.zeros((-used_rows % 16, model_width), bf16),
        ],
        0,
    )
    gathered = doubled(packed, bits)
    gathered, late_features = lax.optimization_barrier((gathered, features))
    for index in (0, 1):
        far_features[index] = passed_along(late_features, shifts[index])
    far_features[2], late_ffn = lax.optimization_barrier((far_features[2], ffn_weights.astype(bf16)))
    low_ffn = lax.all_gather(late_ffn, both, axis=1, tiled=True)
    low_proj = (
        gathered[:, : 5 * shard]
        .reshape(device_count, 5, shard, model_width)
        .transpose(1, 0, 2, 3)
        .reshape(5, model_width, model_width)
    )
    low_vector = (
        gathered[:, 5 * shard, : 8 * shard]
        .reshape(device_count, 8, shard)
        .transpose(1, 0, 2)
        .reshape(8, model_width)
    )
    all_valid = gathered[:, 5 * shard + 1 : used_rows].astype(f32)
    node_total = jnp.sum(all_valid)
    gain_rows = low_vector.astype(f32)

    rank = lax.axis_index("nodes")
    pair = lax.axis_index("fsdp")
    all_valid = all_valid.reshape(device_count, slot_count, block_len)
    far_valid = [
        lax.dynamic_index_in_dim(
            all_valid, ((rank - s) % span_count) * pair_count + pair, 0, keepdims=False
        )
        for s in shifts
    ]
    key_masks = (jnp.concatenate([valid_nodes] + far_valid, 0) - 1.0) * mask_fill
    mask_lines = key_masks[:, None, :]
    mask_cols = jnp.broadcast_to(key_masks[:, :, None], key_masks.shape + (block_len,))

    type_table = gain_rows[7].reshape(NTYPES, H)
    type_onehot = (
        edge_types[:, :, None] == jnp.arange(NTYPES, dtype=jnp.int32)[None, None, :]
    ).astype(f32)
    pair_bias = jnp.einsum("sjt,th->shj", type_onehot, type_table, precision=precise).reshape(-1)
    flat_nbr = neighbours.reshape(-1)

    base, attn_in, queries, own_kv = project(features, low_proj, gain_rows, True)
    far_a1 = []
    far_kv = []
    for piece in far_features:
        a1, kv = project(piece, low_proj, gain_rows, False)
        far_a1.append(a1)
        far_kv.append(kv.reshape(slot_count, block_len, 2 * model_width))
    own_blocks = own_kv.reshape(slot_count, block_len, 2 * model_width)
    query_blocks = queries.reshape(slot_count, block_len, model_width)

    attn_out, lse = attend(flat_nbr, pair_bias, query_blocks, mask_lines, own_blocks, far_kv)
    attn_rows = attn_out.reshape(row_count, model_width)
    attn_y = nn(attn_rows, low_proj[4])
    middle = base + attn_y
    normed_two, norm_two_back = jax.vjp(layer_norm, middle, gain_rows[2], gain_rows[3])
    ffn_in = normed_two.astype(bf16)
    hidden_pre = nn(ffn_in, low_ffn[0])
    hidden_act, gelu_back = jax.vjp(jax.nn.gelu, hidden_pre)
    hidden = hidden_act.astype(bf16)
    ffn_y = nt(hidden, low_ffn[1])
    final = middle + ffn_y
    predict, head_back = jax.vjp(head_out, final, gain_rows[4], gain_rows[5], gain_rows[6])
    error = predict - targets
    local_sums = jnp.stack(
        [jnp.sum(valid_rows * error * error)]
        + [jnp.sum(valid_rows[:, None] * piece * piece) for piece in (middle, attn_y, final, ffn_y)]
    )

    grad_pred = 2.0 * valid_rows * error / node_total
    grad_final, grad_gain_f, grad_shift_f, grad_head = head_back(grad_pred)
    grad_ffn_y = grad_final.astype(bf16)
    grad_down = tn(grad_ffn_y, hidden)
    grad_hidden = nn(grad_ffn_y, low_ffn[1])
    grad_pre = gelu_back(grad_hidden)[0].astype(bf16)
    grad_up = tn(ffn_in, grad_pre)
    order_x, order_y = orders_of(bits)
    split = (device_count, shard, grad_up.shape[1])
    shard_down = halved(grad_down.reshape(split), order_x)
    shard_up = halved(grad_up.reshape(split), order_y)
    grad_ffn_in = nt(grad_pre, low_ffn[0])
    grad_mid_norm, grad_gain_two, grad_shift_two = norm_two_back(grad_ffn_in)
    grad_middle = grad_final + grad_mid_norm
    grad_attn_y = grad_middle.astype(bf16)
    grad_out_proj = tn(attn_rows, grad_attn_y)
    grad_attn = nt(grad_attn_y, low_proj[4]).astype(bf16).reshape(query_blocks.shape)

    head_of = (jnp.arange(model_width)[:, None] // HD == jnp.arange(H)[None, :]).astype(f32)
    inner = lax.dot_general(
        head_of,
        grad_attn.reshape(row_count, model_width).astype(f32) * attn_rows.astype(f32),
        (((0,), (1,)), ((), ())),
        precision=precise,
    )
    inner = inner.reshape(H, slot_count, block_len).transpose(1, 0, 2).reshape(lse.shape)
    low_kv = jnp.concatenate([low_proj[2], low_proj[3]], 1)
    wide = (row_count, 2 * model_width)
    pieces = [None] * 4
    back = [None] * 4
    part_q, far_ab, bias_ab = attend_back(
        flat_nbr, pair_bias, query_blocks, grad_attn, lse, inner, mask_cols, None, None,
        far_kv[2:], 4,
    )
    for index in (3, 2):
        pieces[index] = far_ab[index - 2].reshape(wide)
        ready = nt(pieces[index], low_kv).astype(bf16)
        back[index] = passed_along(ready, -shifts[index])
    grad_q, grad_own, near_ab, bias_near = attend_back(
        flat_nbr, pair_bias, query_blocks, grad_attn, lse, inner, mask_cols, own_blocks, part_q,
        far_kv[:2], 0,
    )
    for index in (0, 1):
        pieces[index] = near_ab[index].reshape(wide)
        ready = nt(pieces[index], low_kv).astype(bf16)
        back[index] = passed_along(ready, -shifts[index])
    grad_bias = jnp.concatenate([bias_near, bias_ab], 1)
    grad_q = grad_q.reshape(row_count, model_width)
    grad_own = grad_own.reshape(wide)
    grad_query_w = tn(attn_in, grad_q)
    grad_kv_w = tn(attn_in, grad_own)
    for index in range(4):
        grad_kv_w = grad_kv_w + tn(far_a1[index], pieces[index])
    split = (device_count, shard, model_width)
    early_a = jnp.concatenate([grad_query_w.reshape(split), grad_out_proj.reshape(split)], 1)
    early_b = grad_kv_w.reshape(device_count, shard, 2 * model_width)
    early_a = halved(early_a, order_x)
    early_b = halved(early_b, order_y)
    grad_attn_in = nt(grad_q, low_proj[1]) + nt(grad_own, low_kv)
    for piece in back:
        grad_attn_in = grad_attn_in + piece.astype(f32)
    _, norm_one_back = jax.vjp(layer_norm, base, gain_rows[0], gain_rows[1])
    grad_base_norm, grad_gain_one, grad_shift_one = norm_one_back(grad_attn_in)
    grad_base = (grad_middle + grad_base_norm).astype(bf16)
    grad_encoder = tn(features, grad_base)
    bias_sums = jnp.sum(grad_bias.reshape(slot_count, listed + 1, H, block_len), -1)
    grad_table = jnp.einsum("sjt,sjh->th", type_onehot, bias_sums, precision=precise)
    vector_rows = [
        grad_gain_one,
        grad_shift_one,
        grad_gain_two,
        grad_shift_two,
        grad_gain_f,
        grad_shift_f,
        grad_head,
        grad_table.reshape(model_width),
    ]
    which = jnp.arange(8)[:, None]
    vector_sum = jnp.zeros((8, model_width), f32)
    for index, row in enumerate(vector_rows):
        vector_sum = jnp.where(which == index, row.reshape(1, model_width), vector_sum)
    for bit in range(bits):
        vector_sum = vector_sum + swap(vector_sum, bit)
    place = lax.axis_index(both)
    shard_vector = lax.dynamic_slice_in_dim(vector_sum, place * shard, shard, 1)
    late = halved(grad_encoder.reshape(split), list(range(bits)))
    shard_proj = jnp.stack(
        [
            late,
            early_a[:shard],
            early_b[:, :model_width],
            early_b[:, model_width:],
            early_a[shard:],
        ]
    )
    shard_ffn = jnp.stack([shard_up, shard_down])

    proj_parts = lamb_parts(proj_weights, shard_proj, proj_mean, proj_square, (1, 2))
    ffn_parts = lamb_parts(ffn_weights, shard_ffn, ffn_mean, ffn_square, (1, 2))
    vector_parts = lamb_parts(vector_params, shard_vector, vector_mean, vector_square, (1,))
    mine = jnp.concatenate(
        [
            proj_parts[3], ffn_parts[3], vector_parts[3],
            proj_parts[4], ffn_parts[4], vector_parts[4],
            local_sums,
        ]
    )
    mine = jnp.pad(mine, (0, 128 - mine.shape[0]))
    everyone = lax.all_to_all(
        jnp.broadcast_to(mine[None], (device_count, 128)), both, 0, 0, tiled=True
    )
    sums = jnp.sum(everyone, 0)
    norm_pairs = jnp.sqrt(jnp.stack([sums[:15], sums[15:30]], 1))
    stat_sums = sums[30:35]
    ratio = norm_pairs[:, 0] / norm_pairs[:, 1]
    updated_proj = proj_weights - learn_rate * ratio[0:5, None, None] * proj_parts[2]
    updated_ffn = ffn_weights - learn_rate * ratio[5:7, None, None] * ffn_parts[2]
    updated_vector = vector_params - learn_rate * ratio[7:15, None] * vector_parts[2]
    train_loss = stat_sums[0] / node_total
    stream_scale = jnp.sqrt(stat_sums[1:] / (node_total * model_width))
    return (
        updated_proj,
        updated_ffn,
        updated_vector,
        proj_parts[0],
        ffn_parts[0],
        vector_parts[0],
        proj_parts[1],
        ffn_parts[1],
        vector_parts[1],
        updated_proj.astype(bf16),
        updated_ffn.astype(bf16),
        updated_vector.astype(bf16),
        norm_pairs,
        stream_scale,
        train_loss,
    )


def solution(mesh):
    rows = P(("nodes", "fsdp"), None)
    line = P(("nodes", "fsdp"))
    cube = P(None, ("nodes", "fsdp"), None)
    flat = P(None, ("nodes", "fsdp"))
    state = (cube, cube, flat)

    return jax.shard_map(
        per_device,
        mesh=mesh,
        in_specs=(rows, line, line, line, rows, rows) + state * 3,
        out_specs=state * 4 + (P(), P(), P()),
        check_vma=False,
    )
```
